32 devices in a mesh: aux: 8 (over z, core), orb: 2 (over y), rep: 2 (over x).
Axes of the slice: x: 2, y: 2, z: 4, core: 2. Of those that a mesh axis runs over, the one named last changes fastest.
Arguments:
- slab: bfloat16 [4096, 4, 1024], P('aux', None, 'orb'), may hold values from -6 to 6
- occ_density: bfloat16 [1024, 512], P('orb'), may hold values from -0.25 to 0.25
- virt_density: bfloat16 [1024, 512], P('orb'), may hold values from -0.25 to 0.25
- block_mask: int32 [32, 8], P('aux', 'orb'), may hold values 0 or 1
- matching: int32 [2, 8], replicated, may hold values from 0 to 7, as said below
Outputs:
- chi_pair: float32 [2, 4096, 512], P('rep', ('aux', 'orb'))
- chi_self: float32 [4096, 512], P(('aux', 'orb'), 'rep')
The draws below stay inside these ranges and needn't reach their ends.
Inputs may be any that keep to these rules, and one draw needn't show every extreme that they name: `matching`: each row pairs the 8 owners: entry p names the partner of p, the partner's entry names p, and no owner is its own partner.
All inputs are finite; a program needn't handle non-finite values. No bound on the sum of `block_mask` on one device may be relied on, other than what follows from the above.
Results may differ from the reference program's by a relative error of at most 0.0041.
Values may be sent and summed in bfloat16 or wider, within the bound.
A program may use at most 64 MiB of HBM per device.

```python
import math
import jax
import jax.numpy as jnp
from jax import lax

BLOCK = 128
AUX_DEV = 512
ORB_DEV = 512
KB = 4
OWNERS = 8
ROUNDS = 2
NAUX = 4096
NORB = 1024
N_ORB = 2


def draw_matching(key, part):
    listed = []
    for round_no in range(ROUNDS):
        shuffled = jax.random.permutation(jax.random.fold_in(key, 11 + round_no), OWNERS).astype(jnp.int32)
        leaders = shuffled[0::2]
        followers = shuffled[1::2]
        partner = jnp.zeros((OWNERS,), jnp.int32).at[leaders].set(followers).at[followers].set(leaders)
        listed.append(partner)
    return jnp.stack(listed).astype(jnp.int32)


def place_ends(entries, stream_key, smallest, top_value):
    longest = entries.shape.index(max(entries.shape))
    spots = []
    for shift in (0, 1):
        where = [jax.random.randint(jax.random.fold_in(stream_key, axis), (), 0, length) for axis, length in enumerate(entries.shape)]
        where[longest] = (where[longest] + shift) % entries.shape[longest]
        spots.append(tuple(where))
    return entries.at[spots[0]].set(smallest).at[spots[1]].set(top_value)


def levels(stream_key, extent, pieces, smallest, top_value):
    level, own = 1.0, jax.random.fold_in(stream_key, 6)
    for dim, blocks in pieces:
        draws = jnp.exp(jax.random.uniform(jax.random.fold_in(own, dim), (blocks,), jnp.float32, smallest / len(pieces), top_value / len(pieces)))
        level = level * jnp.repeat(draws, extent[dim] // blocks).reshape([-1 if axis == dim else 1 for axis in range(len(extent))])
    return level


def centred(own_key, dims, scale, limit, split=(), kind=jnp.bfloat16):
    values = scale * jax.random.normal(own_key, dims, jnp.float32)
    if split:
        values = values * levels(own_key, dims, split, -0.22, 0.18)
    return jnp.clip(values, -limit, limit).astype(kind)


def setup_inputs(seed: int = 0) -> dict:
    seeds = jax.random.split(jax.random.key(seed), 6)
    slab = centred(seeds[0], (NAUX, KB, NORB), 1.0, 6.0, ((0, 8), (2, 2)))
    occ_density = centred(seeds[1], (NORB, ORB_DEV), ORB_DEV ** -0.5, 0.25, ((0, 2),))
    virt_density = centred(seeds[2], (NORB, ORB_DEV), ORB_DEV ** -0.5, 0.25, ((0, 2),))
    block_mask = place_ends((jax.random.randint(seeds[3], (NAUX // BLOCK, NORB // BLOCK), 0, 2) < 1).astype(jnp.int32), jax.random.fold_in(seeds[3], 1), 0, 1)
    matching = draw_matching(jax.random.fold_in(seeds[5], 71), 0)
    return dict(slab=slab, occ_density=occ_density, virt_density=virt_density, block_mask=block_mask, matching=matching)


def transform(density, rows, mask_rows):
    masked = rows * mask_rows[:, None, :]
    blocks = masked.astype(jnp.float32).reshape(AUX_DEV, KB, N_ORB, ORB_DEV)
    dens = density.astype(jnp.float32).reshape(N_ORB, ORB_DEV, ORB_DEV)
    result = jnp.einsum('plbu,but->plbt', blocks, dens)
    return result.reshape(AUX_DEV, KB, NORB).astype(jnp.bfloat16)

def reference(slab, occ_density, virt_density, block_mask, matching):
    factor = 1.0 / math.sqrt(KB * NORB)
    spread = jnp.repeat(jnp.repeat(block_mask.astype(jnp.bfloat16), BLOCK, axis=0), BLOCK, axis=1)
    slab_owned = slab.reshape(OWNERS, AUX_DEV, KB, NORB)
    mask_owned = spread.reshape(OWNERS, AUX_DEV, NORB)
    virtual = lax.map(lambda pair: transform(virt_density, pair[0], pair[1]), (slab_owned, mask_owned))
    virtual = virtual.reshape(OWNERS, AUX_DEV, KB * NORB)

    def one_owner(owner):
        occupied = transform(occ_density, slab_owned[owner], mask_owned[owner]).reshape(AUX_DEV, KB * NORB)
        self_tile = jnp.dot(occupied, virtual[owner].T, preferred_element_type=jnp.float32) * factor

        def round_tile(partner):
            return jnp.dot(occupied, virtual[partner].T, preferred_element_type=jnp.float32) * factor
        pair_tiles = lax.map(round_tile, matching[:, owner])
        return (pair_tiles, self_tile)
    pair_tiles, self_tiles = lax.map(one_owner, jnp.arange(OWNERS, dtype=jnp.int32))
    chi_pair = jnp.transpose(pair_tiles, (1, 0, 2, 3)).reshape(ROUNDS, NAUX, AUX_DEV)
    chi_self = self_tiles.reshape(NAUX, AUX_DEV)
    return (chi_pair, chi_self)
```

```python
import functools
import math

import jax
import jax.numpy as jnp
from jax import lax
from jax.experimental import pallas as pl
from jax.experimental.pallas import tpu as pltpu
from jax.sharding import PartitionSpec as P

BLOCK = 128
MESH = pl.DeviceIdType.MESH
CONTRACT = (((1,), (1,)), ((), ()))


def kernel(sizes, factor, match_ref, masked, occ_dens, virt_dens, pair_out, self_out, *scratch):
    chips, orbs, reps, pieces, groups, rows_piece, half = sizes
    gath = scratch[:pieces]
    (occ, chosen, other, ends, tiles, arrived, self_tile, self_arrived,
     recv_sem, up_sem, down_sem, core_send, core_recv, local_sem, end_send, end_recv,
     rep_send, rep_recv, orb_send, orb_recv) = scratch[pieces:]
    per_group = pieces // groups
    cols_group = per_group * rows_piece
    batch, aux_rows, orb_cols = masked.shape
    rows_out = aux_rows // orbs
    self_cols = aux_rows // reps

    a = lax.axis_index("aux")
    o = lax.axis_index("orb")
    r = lax.axis_index("rep")
    z = a // 2
    k = a % 2
    far = (r + 1) % reps
    inner = jnp.logical_and(z >= 1, z <= chips - 2)
    at_end = jnp.logical_or(z == 0, z == chips - 1)
    up_ok = z + 1 <= chips - 2
    down_ok = z - 1 >= 1
    feeds = jnp.logical_or(z == 1, z == chips - 2)
    end_aux = jnp.where(z == 1, k, 2 * (chips - 1) + k)

    barrier = pltpu.get_barrier_semaphore()

    @pl.when(z > 0)
    def _():
        pl.semaphore_signal(barrier, inc=1, device_id={"aux": a - 2}, device_id_type=MESH)

    @pl.when(z < chips - 1)
    def _():
        pl.semaphore_signal(barrier, inc=1, device_id={"aux": a + 2}, device_id_type=MESH)

    pl.semaphore_signal(barrier, inc=1, device_id={"aux": 2 * z + 1 - k}, device_id_type=MESH)
    pl.semaphore_signal(barrier, inc=1, device_id={"rep": far}, device_id_type=MESH)
    for j in range(1, orbs):
        pl.semaphore_signal(barrier, inc=1, device_id={"orb": (o + j) % orbs}, device_id_type=MESH)
    pl.semaphore_wait(barrier, 2 + orbs - 1 + jnp.where(at_end, 1, 2))

    def piece(c):
        return masked.at[pl.ds(r * half, half), pl.ds(c * rows_piece, rows_piece), :]

    def remote(src, dst, send, recv, where):
        return pltpu.make_async_remote_copy(
            src_ref=src, dst_ref=dst, send_sem=send, recv_sem=recv, device_id=where, device_id_type=MESH
        )

    def slot(c, zz):
        return gath[c].at[2 * zz + k]

    def up(c, zz, src):
        return remote(src, slot(c, zz), up_sem.at[c, zz], recv_sem.at[c, zz], {"aux": a + 2})

    def down(c, zz, src):
        return remote(src, slot(c, zz), down_sem.at[c, zz], recv_sem.at[c, zz], {"aux": a - 2})

    def cross(c, zz, src):
        return remote(src, slot(c, zz), core_send.at[c, zz], core_recv.at[c, zz], {"aux": 2 * z + 1 - k})

    def local(c):
        return pltpu.make_async_copy(piece(c), gath[c].at[a], local_sem.at[c])

    def span(c):
        return c // per_group, pl.ds((c % per_group) * rows_piece, rows_piece)

    def feed(c):
        g, rows = span(c)
        return remote(ends.at[c], chosen.at[g, :, :, rows, :], end_send.at[c], end_recv.at[c], {"aux": end_aux})

    def swap(c):
        g, rows = span(c)
        return remote(chosen.at[g, 1, :, rows, :], other.at[g, :, rows, :], rep_send.at[c], rep_recv.at[c], {"rep": far})

    def lower(c, send):
        for d in range(1, chips):
            @pl.when(z - d >= 0)
            def _():
                zz = jnp.maximum(z - d, 0)
                up(c, zz, slot(c, zz)).wait_recv()
                if send:
                    up(c, zz, slot(c, zz)).start()
                cross(c, zz, slot(c, zz)).start()

    def upper(c, send):
        for d in range(1, chips):
            @pl.when(z + d <= chips - 1)
            def _():
                zz = jnp.minimum(z + d, chips - 1)
                down(c, zz, slot(c, zz)).wait_recv()
                if send:
                    down(c, zz, slot(c, zz)).start()
                cross(c, zz, slot(c, zz)).start()

    def own(c):
        @pl.when(up_ok)
        def _():
            up(c, z, piece(c)).start()

        @pl.when(down_ok)
        def _():
            down(c, z, piece(c)).start()

        @pl.when(inner)
        def _():
            cross(c, z, piece(c)).start()
            local(c).start()

    def relay(c):
        @pl.when(jnp.logical_and(inner, up_ok))
        def _():
            lower(c, True)

        @pl.when(jnp.logical_and(inner, down_ok))
        def _():
            upper(c, True)

    def complete(c):
        g, rows = span(c)

        @pl.when(inner)
        def _():
            @pl.when(jnp.logical_not(up_ok))
            def _():
                lower(c, False)

            @pl.when(jnp.logical_not(down_ok))
            def _():
                upper(c, False)

            for zz in range(chips):
                remote(gath[c].at[2 * zz + k], gath[c].at[2 * zz + 1 - k], core_send.at[c, zz],
                       core_recv.at[c, zz], {"aux": 2 * z + 1 - k}).wait_recv()
            local(c).wait()

            @pl.when(feeds)
            def _():
                ends[c, 0] = gath[c][match_ref[r, end_aux]]
                ends[c, 1] = gath[c][match_ref[far, end_aux]]

            chosen[g, 1, :, rows, :] = gath[c][match_ref[far, a]]
            chosen[g, 0, :, rows, :] = gath[c][match_ref[r, a]]

            @pl.when(feeds)
            def _():
                feed(c).start()

        @pl.when(at_end)
        def _():
            feed(c).wait_recv()

        swap(c).start()

    def orb_copy(g, j):
        peer = (o + j) % orbs
        return remote(tiles.at[g, pl.ds(peer * rows_out, rows_out), :], arrived.at[g, j - 1],
                      orb_send.at[g, j - 1], orb_recv.at[g, j - 1], {"orb": peer})

    def self_copy(j):
        peer = (o + j) % orbs
        return remote(self_tile.at[pl.ds(peer * rows_out, rows_out), :], self_arrived.at[j - 1],
                      orb_send.at[groups, j - 1], orb_recv.at[groups, j - 1], {"orb": peer})

    def product(l, rows_l):
        moved = jnp.dot(rows_l, virt_dens[...], preferred_element_type=jnp.float32).astype(jnp.bfloat16)
        return lax.dot_general(occ[l], moved, CONTRACT, preferred_element_type=jnp.float32)

    def group(g):
        for c in range(g * per_group, (g + 1) * per_group):
            swap(c).wait_recv()
        total = None
        for i in range(half):
            term = product(r * half + i, chosen[g, 0, i])
            total = term if total is None else total + term
            total = total + product(far * half + i, other[g, i])
        tiles[g] = total * factor
        for j in range(1, orbs):
            orb_copy(g, j).start()

    def finish(g):
        total = tiles[g, pl.ds(o * rows_out, rows_out), :]
        for j in range(1, orbs):
            orb_copy(g, j).wait_recv()
            total = total + arrived[g, j - 1]
        pair_out[:, g * cols_group:(g + 1) * cols_group] = total

    own(0)
    own(1)

    def one_occ(l, carry):
        occ[l] = jnp.dot(masked[l], occ_dens[...], preferred_element_type=jnp.float32).astype(jnp.bfloat16)
        return carry

    relay(0)
    lax.fori_loop(0, batch, one_occ, 0)
    for c in range(pieces):
        if c + 2 < pieces:
            own(c + 2)
        if c + 1 < pieces:
            relay(c + 1)
        complete(c)
        if c == 0:
            total = None
            for l in range(batch):
                term = product(l, masked[l, pl.ds(r * self_cols, self_cols), :])
                total = term if total is None else total + term
            self_tile[...] = total * factor
        if c == 1:
            for j in range(1, orbs):
                self_copy(j).start()
        lag = c - 2
        if lag >= 0 and lag % per_group == per_group - 1:
            g = lag // per_group
            group(g)
            if g > 0:
                finish(g - 1)
    done = (pieces - 2) // per_group if pieces > 2 else 0
    for g in range(done, groups):
        group(g)
        if g > 0:
            finish(g - 1)
    total = self_tile[pl.ds(o * rows_out, rows_out), :]
    for j in range(1, orbs):
        self_copy(j).wait_recv()
        total = total + self_arrived[j - 1]
    self_out[...] = total
    finish(groups - 1)

    for c in range(pieces):
        for d in range(chips):
            @pl.when(jnp.logical_and(up_ok, z - d >= 0))
            def _():
                up(c, jnp.maximum(z - d, 0), piece(c)).wait_send()

            @pl.when(jnp.logical_and(down_ok, z + d <= chips - 1))
            def _():
                down(c, jnp.minimum(z + d, chips - 1), piece(c)).wait_send()

        @pl.when(inner)
        def _():
            for zz in range(chips):
                cross(c, zz, piece(c)).wait_send()

        @pl.when(feeds)
        def _():
            feed(c).wait_send()

        swap(c).wait_send()
    for j in range(1, orbs):
        self_copy(j).wait_send()
        for g in range(groups):
            orb_copy(g, j).wait_send()


def per_device(slab, occ_density, virt_density, block_mask, matching):
    owners = lax.axis_size("aux")
    orbs = lax.axis_size("orb")
    reps = lax.axis_size("rep")
    chips = owners // 2
    aux_rows, batch, orb_cols = slab.shape
    pieces = max(2, 32 // chips)
    rows_piece = aux_rows // pieces
    per_group = max(1, BLOCK // rows_piece)
    groups = pieces // per_group
    cols_group = per_group * rows_piece
    half = batch // reps
    rows_out = aux_rows // orbs
    self_cols = aux_rows // reps
    weights = block_mask.astype(jnp.bfloat16)
    spread = jnp.repeat(jnp.repeat(weights, BLOCK, axis=0), BLOCK, axis=1)
    masked = jnp.transpose(slab, (1, 0, 2)) * spread[None]
    factor = 1.0 / math.sqrt(batch * orb_cols * orbs)
    dma = pltpu.SemaphoreType.DMA
    vmem = pl.BlockSpec(memory_space=pltpu.VMEM)
    bf16, f32 = jnp.bfloat16, jnp.float32
    pair, own = pl.pallas_call(
        functools.partial(kernel, (chips, orbs, reps, pieces, groups, rows_piece, half), factor),
        out_shape=(
            jax.ShapeDtypeStruct((rows_out, aux_rows), f32),
            jax.ShapeDtypeStruct((rows_out, self_cols), f32),
        ),
        in_specs=[pl.BlockSpec(memory_space=pltpu.SMEM), vmem, vmem, vmem],
        out_specs=(vmem, vmem),
        scratch_shapes=[pltpu.VMEM((owners, half, rows_piece, orb_cols), bf16) for _ in range(pieces)] + [
            pltpu.VMEM((batch, aux_rows, orb_cols), bf16),
            pltpu.VMEM((groups, 2, half, cols_group, orb_cols), bf16),
            pltpu.VMEM((groups, half, cols_group, orb_cols), bf16),
            pltpu.VMEM((pieces, 2, half, rows_piece, orb_cols), bf16),
            pltpu.VMEM((groups, aux_rows, cols_group), f32),
            pltpu.VMEM((groups, orbs - 1, rows_out, cols_group), f32),
            pltpu.VMEM((aux_rows, self_cols), f32),
            pltpu.VMEM((orbs - 1, rows_out, self_cols), f32),
            dma((pieces, chips)), dma((pieces, chips)), dma((pieces, chips)),
            dma((pieces, chips)), dma((pieces, chips)),
            dma((pieces,)), dma((pieces,)), dma((pieces,)), dma((pieces,)), dma((pieces,)),
            dma((groups + 1, orbs - 1)), dma((groups + 1, orbs - 1)),
        ],
        compiler_params=pltpu.CompilerParams(
            collective_id=0, has_side_effects=True, vmem_limit_bytes=56 * 2**20
        ),
    )(matching, masked, occ_density, virt_density)
    return (pair[None], own)


def solution(mesh):
    return jax.shard_map(
        per_device,
        mesh=mesh,
        in_specs=(P("aux", None, "orb"), P("orb", None), P("orb", None), P("aux", "orb"), P()),
        out_specs=(P("rep", ("aux", "orb"), None), P(("aux", "orb"), "rep")),
        check_vma=False,
    )
```

```python
import functools
import math

import jax
import jax.numpy as jnp
from jax import lax
from jax.experimental import pallas as pl
from jax.experimental.pallas import tpu as pltpu
from jax.sharding import PartitionSpec as P

BLOCK = 128
MESH = pl.DeviceIdType.MESH
CONTRACT = (((1,), (1,)), ((), ()))


def kernel(sizes, factor, match_ref, masked, occ_dens, virt_dens, pair_out, self_out, *scratch):
    chips, orbs, reps, pieces, groups, rows_piece, half = sizes
    gath = scratch[:pieces]
    (occ, parts, whole, arrived, ends, landed, self_tile, self_arrived,
     recv_sem, up_sem, down_sem, core_send, core_recv, local_sem, end_send, end_recv,
     part_send, part_recv, self_send, self_recv) = scratch[pieces:]
    per_group = pieces // groups
    cols_group = per_group * rows_piece
    batch, aux_rows, orb_cols = masked.shape
    rows_out = aux_rows // orbs
    self_cols = aux_rows // reps

    a = lax.axis_index("aux")
    o = lax.axis_index("orb")
    r = lax.axis_index("rep")
    z = a // 2
    k = a % 2

    def peer(j):
        to_orb, to_rep = (o + j // reps) % orbs, (r + j % reps) % reps
        return to_orb, to_rep, {"orb": to_orb, "rep": to_rep}

    inner = jnp.logical_and(z >= 1, z <= chips - 2)
    at_end = jnp.logical_or(z == 0, z == chips - 1)
    up_ok = z + 1 <= chips - 2
    down_ok = z - 1 >= 1
    feeds = jnp.logical_or(z == 1, z == chips - 2)
    end_aux = jnp.where(z == 1, k, 2 * (chips - 1) + k)

    barrier = pltpu.get_barrier_semaphore()

    @pl.when(z > 0)
    def _():
        pl.semaphore_signal(barrier, inc=1, device_id={"aux": a - 2}, device_id_type=MESH)

    @pl.when(z < chips - 1)
    def _():
        pl.semaphore_signal(barrier, inc=1, device_id={"aux": a + 2}, device_id_type=MESH)

    pl.semaphore_signal(barrier, inc=1, device_id={"aux": 2 * z + 1 - k}, device_id_type=MESH)
    for j in range(1, orbs * reps):
        pl.semaphore_signal(barrier, inc=1, device_id=peer(j)[2], device_id_type=MESH)
    pl.semaphore_wait(barrier, orbs * reps + jnp.where(at_end, 1, 2))

    def piece(c):
        return masked.at[pl.ds(r * half, half), pl.ds(c * rows_piece, rows_piece), :]

    def remote(src, dst, send, recv, where):
        return pltpu.make_async_remote_copy(
            src_ref=src, dst_ref=dst, send_sem=send, recv_sem=recv, device_id=where, device_id_type=MESH
        )

    def slot(c, zz):
        return gath[c].at[2 * zz + k]

    def up(c, zz, src):
        return remote(src, slot(c, zz), up_sem.at[c, zz], recv_sem.at[c, zz], {"aux": a + 2})

    def down(c, zz, src):
        return remote(src, slot(c, zz), down_sem.at[c, zz], recv_sem.at[c, zz], {"aux": a - 2})

    def cross(c, zz, src):
        return remote(src, slot(c, zz), core_send.at[c, zz], core_recv.at[c, zz], {"aux": 2 * z + 1 - k})

    def local(c):
        return pltpu.make_async_copy(piece(c), gath[c].at[a], local_sem.at[c])

    def lower(c, send):
        for d in range(1, chips):
            @pl.when(z - d >= 0)
            def _():
                zz = jnp.maximum(z - d, 0)
                up(c, zz, slot(c, zz)).wait_recv()
                if send:
                    up(c, zz, slot(c, zz)).start()
                cross(c, zz, slot(c, zz)).start()

    def upper(c, send):
        for d in range(1, chips):
            @pl.when(z + d <= chips - 1)
            def _():
                zz = jnp.minimum(z + d, chips - 1)
                down(c, zz, slot(c, zz)).wait_recv()
                if send:
                    down(c, zz, slot(c, zz)).start()
                cross(c, zz, slot(c, zz)).start()

    def own(c):
        @pl.when(up_ok)
        def _():
            up(c, z, piece(c)).start()

        @pl.when(down_ok)
        def _():
            down(c, z, piece(c)).start()

        @pl.when(inner)
        def _():
            cross(c, z, piece(c)).start()
            local(c).start()

    def relay(c):
        @pl.when(jnp.logical_and(inner, up_ok))
        def _():
            lower(c, True)

        @pl.when(jnp.logical_and(inner, down_ok))
        def _():
            upper(c, True)

    def complete(c):
        @pl.when(inner)
        def _():
            @pl.when(jnp.logical_not(up_ok))
            def _():
                lower(c, False)

            @pl.when(jnp.logical_not(down_ok))
            def _():
                upper(c, False)

    def part_copy(g, t, j):
        to_orb, to_rep, where = peer(j)
        return remote(parts.at[g, t, to_rep, pl.ds(to_orb * rows_out, rows_out), :], arrived.at[g, t, j - 1],
                      part_send.at[g, t, j - 1], part_recv.at[g, t, j - 1], where)

    def feed(g):
        return remote(ends.at[g], landed.at[g], end_send.at[g], end_recv.at[g], {"aux": end_aux})

    def self_copy(j):
        to_orb = (o + j) % orbs
        return remote(self_tile.at[pl.ds(to_orb * rows_out, rows_out), :], self_arrived.at[j - 1],
                      self_send.at[j - 1], self_recv.at[j - 1], {"orb": to_orb})

    def product(l, rows_l):
        moved = jnp.dot(rows_l, virt_dens[...], preferred_element_type=jnp.float32).astype(jnp.bfloat16)
        return lax.dot_general(occ[l], moved, CONTRACT, preferred_element_type=jnp.float32)

    def end_occ(c):
        @pl.when(feeds)
        def _():
            rows_e = gath[c][end_aux].reshape(half * rows_piece, orb_cols)
            made = jnp.dot(rows_e, occ_dens[...], preferred_element_type=jnp.float32).astype(jnp.bfloat16)
            occ[batch:, c * rows_piece:(c + 1) * rows_piece, :] = made.reshape(half, rows_piece, orb_cols)

    def group(g):
        span = range(g * per_group, (g + 1) * per_group)

        @pl.when(inner)
        def _():
            for c in span:
                for zz in range(chips):
                    remote(gath[c].at[2 * zz + k], gath[c].at[2 * zz + 1 - k], core_send.at[c, zz],
                           core_recv.at[c, zz], {"aux": 2 * z + 1 - k}).wait_recv()
                local(c).wait()

            def one_tile(n, carry):
                t, turn = n // reps, n % reps
                owner = jnp.where(t == 0, a, end_aux)
                first = jnp.where(t == 0, r * half, batch)
                partner = match_ref[turn, owner]
                total = None
                for i in range(half):
                    rows_l = [gath[c][partner, i] for c in span]
                    rows_l = rows_l[0] if per_group == 1 else jnp.concatenate(rows_l, 0)
                    term = product(first + i, rows_l)
                    total = term if total is None else total + term
                total = total * factor
                parts[g, t, turn] = total.astype(jnp.bfloat16)
                whole[g, t, turn] = total
                return carry

            lax.fori_loop(0, jnp.where(feeds, 2 * reps, reps), one_tile, 0)
            for j in range(1, orbs * reps):
                @pl.when(feeds)
                def _():
                    part_copy(g, 1, j).start()
            for j in range(1, orbs * reps):
                part_copy(g, 0, j).start()

    def summed(g, t):
        total = whole[g, t, r, pl.ds(o * rows_out, rows_out), :]
        for j in range(1, orbs * reps):
            part_copy(g, t, j).wait_recv()
            total = total + arrived[g, t, j - 1].astype(jnp.float32)
        return total

    def finish(g):
        @pl.when(inner)
        def _():
            @pl.when(feeds)
            def _():
                ends[g] = summed(g, 1)
                feed(g).start()

            pair_out[:, g * cols_group:(g + 1) * cols_group] = summed(g, 0)

    ahead = 2
    ready = 0
    closed = 0

    def one_occ(l, carry):
        occ[l] = jnp.dot(masked[l], occ_dens[...], preferred_element_type=jnp.float32).astype(jnp.bfloat16)
        return carry

    own(0)
    own(1)
    lax.fori_loop(0, batch, one_occ, 0)
    for c in range(min(ahead, pieces)):
        relay(c)
        end_occ(c)
    for c in range(pieces):
        if c + 2 < pieces:
            own(c + 2)
        if c + ahead < pieces:
            relay(c + ahead)
            end_occ(c + ahead)
        filled = c + ahead >= pieces - 1
        if filled and (ready + 1) * per_group <= c:
            group(ready)
            ready += 1
        complete(c)
        if c == 0:
            total = None
            for l in range(batch):
                term = product(l, masked[l, pl.ds(r * self_cols, self_cols), :])
                total = term if total is None else total + term
            self_tile[...] = total * factor
        if c == 1:
            for j in range(1, orbs):
                self_copy(j).start()
        if filled and c == pieces - 2 and closed + 1 < ready:
            finish(closed)
            closed += 1
        if filled and c < pieces - 1 and (ready + 1) * per_group <= c + 1:
            group(ready)
            ready += 1
    for g in range(ready, groups):
        group(g)
    total = self_tile[pl.ds(o * rows_out, rows_out), :]
    for j in range(1, orbs):
        self_copy(j).wait_recv()
        total = total + self_arrived[j - 1]
    self_out[...] = total
    for g in range(closed, groups):
        finish(g)

    @pl.when(at_end)
    def _():
        for g in range(groups):
            feed(g).wait_recv()
            pair_out[:, g * cols_group:(g + 1) * cols_group] = landed[g]

    for c in range(pieces):
        for d in range(chips):
            @pl.when(jnp.logical_and(up_ok, z - d >= 0))
            def _():
                up(c, jnp.maximum(z - d, 0), piece(c)).wait_send()

            @pl.when(jnp.logical_and(down_ok, z + d <= chips - 1))
            def _():
                down(c, jnp.minimum(z + d, chips - 1), piece(c)).wait_send()

        @pl.when(inner)
        def _():
            for zz in range(chips):
                cross(c, zz, piece(c)).wait_send()

    for j in range(1, orbs):
        self_copy(j).wait_send()
    for g in range(groups):
        @pl.when(inner)
        def _():
            for j in range(1, orbs * reps):
                part_copy(g, 0, j).wait_send()

        @pl.when(feeds)
        def _():
            for j in range(1, orbs * reps):
                part_copy(g, 1, j).wait_send()
            feed(g).wait_send()


def per_device(slab, occ_density, virt_density, block_mask, matching):
    owners = lax.axis_size("aux")
    orbs = lax.axis_size("orb")
    reps = lax.axis_size("rep")
    chips = owners // 2
    aux_rows, batch, orb_cols = slab.shape
    pieces = max(2, 32 // chips)
    rows_piece = aux_rows // pieces
    per_group = max(1, BLOCK // rows_piece)
    groups = pieces // per_group
    cols_group = per_group * rows_piece
    half = batch // reps
    rows_out = aux_rows // orbs
    self_cols = aux_rows // reps
    weights = block_mask.astype(jnp.bfloat16)
    spread = jnp.repeat(jnp.repeat(weights, BLOCK, axis=0), BLOCK, axis=1)
    masked = jnp.transpose(slab, (1, 0, 2)) * spread[None]
    factor = 1.0 / math.sqrt(batch * orb_cols * orbs)
    dma = pltpu.SemaphoreType.DMA
    vmem = pl.BlockSpec(memory_space=pltpu.VMEM)
    bf16, f32 = jnp.bfloat16, jnp.float32
    pair, own = pl.pallas_call(
        functools.partial(kernel, (chips, orbs, reps, pieces, groups, rows_piece, half), factor),
        out_shape=(
            jax.ShapeDtypeStruct((rows_out, aux_rows), f32),
            jax.ShapeDtypeStruct((rows_out, self_cols), f32),
        ),
        in_specs=[pl.BlockSpec(memory_space=pltpu.SMEM), vmem, vmem, vmem],
        out_specs=(vmem, vmem),
        scratch_shapes=[pltpu.VMEM((owners, half, rows_piece, orb_cols), bf16) for _ in range(pieces)] + [
            pltpu.VMEM((batch + half, aux_rows, orb_cols), bf16),
            pltpu.VMEM((groups, 2, reps, aux_rows, cols_group), bf16),
            pltpu.VMEM((groups, 2, reps, aux_rows, cols_group), f32),
            pltpu.VMEM((groups, 2, orbs * reps - 1, rows_out, cols_group), bf16),
            pltpu.VMEM((groups, rows_out, cols_group), f32),
            pltpu.VMEM((groups, rows_out, cols_group), f32),
            pltpu.VMEM((aux_rows, self_cols), f32),
            pltpu.VMEM((orbs - 1, rows_out, self_cols), f32),
            dma((pieces, chips)), dma((pieces, chips)), dma((pieces, chips)),
            dma((pieces, chips)), dma((pieces, chips)),
            dma((pieces,)), dma((groups,)), dma((groups,)),
            dma((groups, 2, orbs * reps - 1)), dma((groups, 2, orbs * reps - 1)),
            dma((orbs - 1,)), dma((orbs - 1,)),
        ],
        compiler_params=pltpu.CompilerParams(
            collective_id=0, has_side_effects=True, vmem_limit_bytes=56 * 2**20
        ),
    )(matching, masked, occ_density, virt_density)
    return (pair[None], own)


def solution(mesh):
    return jax.shard_map(
        per_device,
        mesh=mesh,
        in_specs=(P("aux", None, "orb"), P("orb", None), P("orb", None), P("aux", "orb"), P()),
        out_specs=(P("rep", ("aux", "orb"), None), P(("aux", "orb"), "rep")),
        check_vma=False,
    )
```

```python
import functools
import math

import jax
import jax.numpy as jnp
from jax import lax
from jax.experimental import pallas as pl
from jax.experimental.pallas import tpu as pltpu
from jax.sharding import PartitionSpec as P

BLOCK = 128
MESH = pl.DeviceIdType.MESH
CONTRACT = (((1,), (1,)), ((), ()))


def kernel(sizes, factor, match_ref, masked, occ_dens, virt_dens, pair_out, self_out, *scratch):
    chips, orbs, reps, pieces, groups, rows_piece, half = sizes
    gath = scratch[:pieces]
    (occ, parts, whole, arrived, ends, landed, self_tile, self_arrived,
     recv_sem, up_sem, down_sem, core_send, core_recv, local_sem, end_send, end_recv,
     part_send, part_recv, self_send, self_recv) = scratch[pieces:]
    per_group = pieces // groups
    cols_group = per_group * rows_piece
    batch, aux_rows, orb_cols = masked.shape
    rows_out = aux_rows // orbs
    self_cols = aux_rows // reps

    a = lax.axis_index("aux")
    o = lax.axis_index("orb")
    r = lax.axis_index("rep")
    z = a // 2
    k = a % 2

    def peer(j):
        to_orb, to_rep = (o + j // reps) % orbs, (r + j % reps) % reps
        return to_orb, to_rep, {"orb": to_orb, "rep": to_rep}

    inner = jnp.logical_and(z >= 1, z <= chips - 2)
    at_end = jnp.logical_or(z == 0, z == chips - 1)
    up_ok = z + 1 <= chips - 2
    down_ok = z - 1 >= 1
    feeds = jnp.logical_or(z == 1, z == chips - 2)
    end_aux = jnp.where(z == 1, k, 2 * (chips - 1) + k)

    barrier = pltpu.get_barrier_semaphore()

    @pl.when(z > 0)
    def _():
        pl.semaphore_signal(barrier, inc=1, device_id={"aux": a - 2}, device_id_type=MESH)

    @pl.when(z < chips - 1)
    def _():
        pl.semaphore_signal(barrier, inc=1, device_id={"aux": a + 2}, device_id_type=MESH)

    pl.semaphore_signal(barrier, inc=1, device_id={"aux": 2 * z + 1 - k}, device_id_type=MESH)
    for j in range(1, orbs * reps):
        pl.semaphore_signal(barrier, inc=1, device_id=peer(j)[2], device_id_type=MESH)
    pl.semaphore_wait(barrier, orbs * reps + jnp.where(at_end, 1, 2))

    def piece(c):
        return masked.at[pl.ds(r * half, half), pl.ds(c * rows_piece, rows_piece), :]

    def remote(src, dst, send, recv, where):
        return pltpu.make_async_remote_copy(
            src_ref=src, dst_ref=dst, send_sem=send, recv_sem=recv, device_id=where, device_id_type=MESH
        )

    def slot(c, zz):
        return gath[c].at[2 * zz + k]

    def up(c, zz, src):
        return remote(src, slot(c, zz), up_sem.at[c, zz], recv_sem.at[c, zz], {"aux": a + 2})

    def down(c, zz, src):
        return remote(src, slot(c, zz), down_sem.at[c, zz], recv_sem.at[c, zz], {"aux": a - 2})

    def cross(c, zz, src):
        return remote(src, slot(c, zz), core_send.at[c, zz], core_recv.at[c, zz], {"aux": 2 * z + 1 - k})

    def local(c):
        return pltpu.make_async_copy(piece(c), gath[c].at[a], local_sem.at[c])

    def lower(c, send):
        for d in range(1, chips):
            @pl.when(z - d >= 0)
            def _():
                zz = jnp.maximum(z - d, 0)
                up(c, zz, slot(c, zz)).wait_recv()
                if send:
                    up(c, zz, slot(c, zz)).start()
                cross(c, zz, slot(c, zz)).start()

    def upper(c, send):
        for d in range(1, chips):
            @pl.when(z + d <= chips - 1)
            def _():
                zz = jnp.minimum(z + d, chips - 1)
                down(c, zz, slot(c, zz)).wait_recv()
                if send:
                    down(c, zz, slot(c, zz)).start()
                cross(c, zz, slot(c, zz)).start()

    def own(c):
        @pl.when(up_ok)
        def _():
            up(c, z, piece(c)).start()

        @pl.when(down_ok)
        def _():
            down(c, z, piece(c)).start()

        @pl.when(inner)
        def _():
            cross(c, z, piece(c)).start()
            local(c).start()

    def relay(c):
        @pl.when(jnp.logical_and(inner, up_ok))
        def _():
            lower(c, True)

        @pl.when(jnp.logical_and(inner, down_ok))
        def _():
            upper(c, True)

    def complete(c):
        @pl.when(inner)
        def _():
            @pl.when(jnp.logical_not(up_ok))
            def _():
                lower(c, False)

            @pl.when(jnp.logical_not(down_ok))
            def _():
                upper(c, False)

    def part_copy(g, t, j):
        to_orb, to_rep, where = peer(j)
        return remote(parts.at[g, t, to_rep, pl.ds(to_orb * rows_out, rows_out), :], arrived.at[g, t, j - 1],
                      part_send.at[g, t, j - 1], part_recv.at[g, t, j - 1], where)

    def feed(g):
        return remote(ends.at[g], landed.at[g], end_send.at[g], end_recv.at[g], {"aux": end_aux})

    def self_copy(j):
        to_orb = (o + j) % orbs
        return remote(self_tile.at[pl.ds(to_orb * rows_out, rows_out), :], self_arrived.at[j - 1],
                      self_send.at[j - 1], self_recv.at[j - 1], {"orb": to_orb})

    def product(l, rows_l):
        moved = jnp.dot(rows_l, virt_dens[...], preferred_element_type=jnp.float32).astype(jnp.bfloat16)
        return lax.dot_general(occ[l], moved, CONTRACT, preferred_element_type=jnp.float32)

    def end_occ(c):
        @pl.when(feeds)
        def _():
            rows_e = gath[c][end_aux].reshape(half * rows_piece, orb_cols)
            made = jnp.dot(rows_e, occ_dens[...], preferred_element_type=jnp.float32).astype(jnp.bfloat16)
            occ[batch:, c * rows_piece:(c + 1) * rows_piece, :] = made.reshape(half, rows_piece, orb_cols)

    def group(g):
        span = range(g * per_group, (g + 1) * per_group)

        @pl.when(inner)
        def _():
            for c in span:
                for zz in range(chips):
                    remote(gath[c].at[2 * zz + k], gath[c].at[2 * zz + 1 - k], core_send.at[c, zz],
                           core_recv.at[c, zz], {"aux": 2 * z + 1 - k}).wait_recv()
                local(c).wait()

            def one_tile(n, carry):
                t, turn = n // reps, n % reps
                owner = jnp.where(t == 0, a, end_aux)
                first = jnp.where(t == 0, r * half, batch)
                partner = match_ref[turn, owner]
                total = None
                for i in range(half):
                    rows_l = [gath[c][partner, i] for c in span]
                    rows_l = rows_l[0] if per_group == 1 else jnp.concatenate(rows_l, 0)
                    term = product(first + i, rows_l)
                    total = term if total is None else total + term
                total = total * factor
                parts[g, t, turn] = total.astype(jnp.bfloat16)
                whole[g, t, turn] = total
                return carry

            lax.fori_loop(0, jnp.where(feeds, 2 * reps, reps), one_tile, 0)
            for j in range(1, orbs * reps):
                @pl.when(feeds)
                def _():
                    part_copy(g, 1, j).start()
            for j in range(1, orbs * reps):
                part_copy(g, 0, j).start()

    def summed(g, t):
        total = whole[g, t, r, pl.ds(o * rows_out, rows_out), :]
        for j in range(1, orbs * reps):
            part_copy(g, t, j).wait_recv()
            total = total + arrived[g, t, j - 1].astype(jnp.float32)
        return total

    def finish(g):
        @pl.when(inner)
        def _():
            @pl.when(feeds)
            def _():
                ends[g] = summed(g, 1)
                feed(g).start()

            pair_out[:, g * cols_group:(g + 1) * cols_group] = summed(g, 0)

    ahead = min(4, pieces)
    ready = 0
    closed = 0

    def one_occ(l, carry):
        occ[l] = jnp.dot(masked[l], occ_dens[...], preferred_element_type=jnp.float32).astype(jnp.bfloat16)
        return carry

    own(0)
    own(1)
    lax.fori_loop(0, batch, one_occ, 0)
    total = None
    for l in range(batch):
        term = product(l, masked[l, pl.ds(r * self_cols, self_cols), :])
        total = term if total is None else total + term
    self_tile[...] = total * factor
    for c in range(ahead):
        if c + 2 < pieces:
            own(c + 2)
        relay(c)
        end_occ(c)
        if c == 0:
            for j in range(1, orbs):
                self_copy(j).start()
    for c in range(pieces):
        if c + ahead + 2 < pieces:
            own(c + ahead + 2)
        if c + ahead < pieces:
            relay(c + ahead)
            end_occ(c + ahead)
        filled = c + ahead >= pieces - 1
        if filled and (ready + 1) * per_group <= c:
            group(ready)
            ready += 1
        complete(c)
        if filled and c == pieces - 2 and closed + 1 < ready:
            finish(closed)
            closed += 1
        if filled and c < pieces - 1 and (ready + 1) * per_group <= c + 1:
            group(ready)
            ready += 1
    for g in range(ready, groups):
        group(g)
    total = self_tile[pl.ds(o * rows_out, rows_out), :]
    for j in range(1, orbs):
        self_copy(j).wait_recv()
        total = total + self_arrived[j - 1]
    self_out[...] = total
    for g in range(closed, groups):
        finish(g)

    @pl.when(at_end)
    def _():
        for g in range(groups):
            feed(g).wait_recv()
            pair_out[:, g * cols_group:(g + 1) * cols_group] = landed[g]

    for c in range(pieces):
        for d in range(chips):
            @pl.when(jnp.logical_and(up_ok, z - d >= 0))
            def _():
                up(c, jnp.maximum(z - d, 0), piece(c)).wait_send()

            @pl.when(jnp.logical_and(down_ok, z + d <= chips - 1))
            def _():
                down(c, jnp.minimum(z + d, chips - 1), piece(c)).wait_send()

        @pl.when(inner)
        def _():
            for zz in range(chips):
                cross(c, zz, piece(c)).wait_send()

    for j in range(1, orbs):
        self_copy(j).wait_send()
    for g in range(groups):
        @pl.when(inner)
        def _():
            for j in range(1, orbs * reps):
                part_copy(g, 0, j).wait_send()

        @pl.when(feeds)
        def _():
            for j in range(1, orbs * reps):
                part_copy(g, 1, j).wait_send()
            feed(g).wait_send()


def per_device(slab, occ_density, virt_density, block_mask, matching):
    owners = lax.axis_size("aux")
    orbs = lax.axis_size("orb")
    reps = lax.axis_size("rep")
    chips = owners // 2
    aux_rows, batch, orb_cols = slab.shape
    pieces = max(2, 32 // chips)
    rows_piece = aux_rows // pieces
    per_group = max(1, BLOCK // rows_piece)
    groups = pieces // per_group
    cols_group = per_group * rows_piece
    half = batch // reps
    rows_out = aux_rows // orbs
    self_cols = aux_rows // reps
    spread = jnp.repeat(jnp.repeat(block_mask, BLOCK, axis=0), BLOCK, axis=1)
    masked = jnp.transpose(slab, (1, 0, 2)) * spread.astype(jnp.bfloat16)[None]
    factor = 1.0 / math.sqrt(batch * orb_cols * orbs)
    dma = pltpu.SemaphoreType.DMA
    vmem = pl.BlockSpec(memory_space=pltpu.VMEM)
    bf16, f32 = jnp.bfloat16, jnp.float32
    pair, own = pl.pallas_call(
        functools.partial(kernel, (chips, orbs, reps, pieces, groups, rows_piece, half), factor),
        out_shape=(
            jax.ShapeDtypeStruct((rows_out, aux_rows), f32),
            jax.ShapeDtypeStruct((rows_out, self_cols), f32),
        ),
        in_specs=[pl.BlockSpec(memory_space=pltpu.SMEM), vmem, vmem, vmem],
        out_specs=(vmem, vmem),
        scratch_shapes=[pltpu.VMEM((owners, half, rows_piece, orb_cols), bf16) for _ in range(pieces)] + [
            pltpu.VMEM((batch + half, aux_rows, orb_cols), bf16),
            pltpu.VMEM((groups, 2, reps, aux_rows, cols_group), bf16),
            pltpu.VMEM((groups, 2, reps, aux_rows, cols_group), f32),
            pltpu.VMEM((groups, 2, orbs * reps - 1, rows_out, cols_group), bf16),
            pltpu.VMEM((groups, rows_out, cols_group), f32),
            pltpu.VMEM((groups, rows_out, cols_group), f32),
            pltpu.VMEM((aux_rows, self_cols), f32),
            pltpu.VMEM((orbs - 1, rows_out, self_cols), f32),
            dma((pieces, chips)), dma((pieces, chips)), dma((pieces, chips)),
            dma((pieces, chips)), dma((pieces, chips)),
            dma((pieces,)), dma((groups,)), dma((groups,)),
            dma((groups, 2, orbs * reps - 1)), dma((groups, 2, orbs * reps - 1)),
            dma((orbs - 1,)), dma((orbs - 1,)),
        ],
        compiler_params=pltpu.CompilerParams(
            collective_id=0, has_side_effects=True, vmem_limit_bytes=56 * 2**20
        ),
    )(matching, masked, occ_density, virt_density)
    return (pair[None], own)


def solution(mesh):
    return jax.shard_map(
        per_device,
        mesh=mesh,
        in_specs=(P("aux", None, "orb"), P("orb", None), P("orb", None), P("aux", "orb"), P()),
        out_specs=(P("rep", ("aux", "orb"), None), P(("aux", "orb"), "rep")),
        check_vma=False,
    )
```

```python
import functools
import math

import jax
import jax.numpy as jnp
from jax import lax
from jax.experimental import pallas as pl
from jax.experimental.pallas import tpu as pltpu
from jax.sharding import PartitionSpec as P

BLOCK = 128
MESH = pl.DeviceIdType.MESH
CONTRACT = (((1,), (1,)), ((), ()))


def kernel(sizes, factor, match_ref, masked, occ_dens, virt_dens, pair_out, self_out, *scratch):
    chips, orbs, reps, pieces, groups, rows_piece, half = sizes
    gath = scratch[:pieces]
    (occ, parts, whole, arrived, ends, landed, self_tile, self_arrived,
     recv_sem, up_sem, down_sem, core_send, core_recv, local_sem, end_send, end_recv,
     part_send, part_recv, self_send, self_recv) = scratch[pieces:]
    per_group = pieces // groups
    cols_group = per_group * rows_piece
    batch, aux_rows, orb_cols = masked.shape
    rows_out = aux_rows // orbs
    self_cols = aux_rows // reps

    a = lax.axis_index("aux")
    o = lax.axis_index("orb")
    r = lax.axis_index("rep")
    z = a // 2
    k = a % 2

    def peer(j):
        to_orb, to_rep = (o + j // reps) % orbs, (r + j % reps) % reps
        return to_orb, to_rep, {"orb": to_orb, "rep": to_rep}

    inner = jnp.logical_and(z >= 1, z <= chips - 2)
    at_end = jnp.logical_or(z == 0, z == chips - 1)
    up_ok = z + 1 <= chips - 2
    down_ok = z - 1 >= 1
    feeds = jnp.logical_or(z == 1, z == chips - 2)
    end_aux = jnp.where(z == 1, k, 2 * (chips - 1) + k)

    barrier = pltpu.get_barrier_semaphore()

    @pl.when(z > 0)
    def _():
        pl.semaphore_signal(barrier, inc=1, device_id={"aux": a - 2}, device_id_type=MESH)

    @pl.when(z < chips - 1)
    def _():
        pl.semaphore_signal(barrier, inc=1, device_id={"aux": a + 2}, device_id_type=MESH)

    pl.semaphore_signal(barrier, inc=1, device_id={"aux": 2 * z + 1 - k}, device_id_type=MESH)
    for j in range(1, orbs * reps):
        pl.semaphore_signal(barrier, inc=1, device_id=peer(j)[2], device_id_type=MESH)
    pl.semaphore_wait(barrier, orbs * reps + jnp.where(at_end, 1, 2))

    def piece(c):
        return masked.at[pl.ds(r * half, half), pl.ds(c * rows_piece, rows_piece), :]

    def remote(src, dst, send, recv, where):
        return pltpu.make_async_remote_copy(
            src_ref=src, dst_ref=dst, send_sem=send, recv_sem=recv, device_id=where, device_id_type=MESH
        )

    def slot(c, zz):
        return gath[c].at[2 * zz + k]

    def up(c, zz, src):
        return remote(src, slot(c, zz), up_sem.at[c, zz], recv_sem.at[c, zz], {"aux": a + 2})

    def down(c, zz, src):
        return remote(src, slot(c, zz), down_sem.at[c, zz], recv_sem.at[c, zz], {"aux": a - 2})

    def cross(c, zz, src):
        return remote(src, slot(c, zz), core_send.at[c, zz], core_recv.at[c, zz], {"aux": 2 * z + 1 - k})

    def local(c):
        return pltpu.make_async_copy(piece(c), gath[c].at[a], local_sem.at[c])

    def lower(c, send):
        for d in range(1, chips):
            @pl.when(z - d >= 0)
            def _():
                zz = jnp.maximum(z - d, 0)
                up(c, zz, slot(c, zz)).wait_recv()
                if send:
                    up(c, zz, slot(c, zz)).start()
                cross(c, zz, slot(c, zz)).start()

    def upper(c, send):
        for d in range(1, chips):
            @pl.when(z + d <= chips - 1)
            def _():
                zz = jnp.minimum(z + d, chips - 1)
                down(c, zz, slot(c, zz)).wait_recv()
                if send:
                    down(c, zz, slot(c, zz)).start()
                cross(c, zz, slot(c, zz)).start()

    def own(c):
        @pl.when(up_ok)
        def _():
            up(c, z, piece(c)).start()

        @pl.when(down_ok)
        def _():
            down(c, z, piece(c)).start()

        @pl.when(inner)
        def _():
            cross(c, z, piece(c)).start()
            local(c).start()

    def relay(c):
        @pl.when(jnp.logical_and(inner, up_ok))
        def _():
            lower(c, True)

        @pl.when(jnp.logical_and(inner, down_ok))
        def _():
            upper(c, True)

    def complete(c):
        @pl.when(inner)
        def _():
            @pl.when(jnp.logical_not(up_ok))
            def _():
                lower(c, False)

            @pl.when(jnp.logical_not(down_ok))
            def _():
                upper(c, False)

    def part_copy(g, t, j):
        to_orb, to_rep, where = peer(j)
        return remote(parts.at[g, t, to_rep, pl.ds(to_orb * rows_out, rows_out), :], arrived.at[g, t, j - 1],
                      part_send.at[g, t, j - 1], part_recv.at[g, t, j - 1], where)

    def feed(g):
        return remote(ends.at[g], landed.at[g], end_send.at[g], end_recv.at[g], {"aux": end_aux})

    def self_copy(j):
        to_orb = (o + j) % orbs
        return remote(self_tile.at[pl.ds(to_orb * rows_out, rows_out), :], self_arrived.at[j - 1],
                      self_send.at[j - 1], self_recv.at[j - 1], {"orb": to_orb})

    def product(l, rows_l):
        moved = jnp.dot(rows_l, virt_dens[...], preferred_element_type=jnp.float32).astype(jnp.bfloat16)
        return lax.dot_general(occ[l], moved, CONTRACT, preferred_element_type=jnp.float32)

    def end_occ(c):
        @pl.when(feeds)
        def _():
            rows_e = gath[c][end_aux].reshape(half * rows_piece, orb_cols)
            made = jnp.dot(rows_e, occ_dens[...], preferred_element_type=jnp.float32).astype(jnp.bfloat16)
            occ[batch:, c * rows_piece:(c + 1) * rows_piece, :] = made.reshape(half, rows_piece, orb_cols)

    def group(g):
        span = range(g * per_group, (g + 1) * per_group)

        @pl.when(inner)
        def _():
            for c in span:
                for zz in range(chips):
                    remote(gath[c].at[2 * zz + k], gath[c].at[2 * zz + 1 - k], core_send.at[c, zz],
                           core_recv.at[c, zz], {"aux": 2 * z + 1 - k}).wait_recv()
                local(c).wait()

            def one_tile(n, carry):
                t, turn = n // reps, n % reps
                owner = jnp.where(t == 0, a, end_aux)
                first = jnp.where(t == 0, r * half, batch)
                partner = match_ref[turn, owner]
                total = None
                for i in range(half):
                    rows_l = [gath[c][partner, i] for c in span]
                    rows_l = rows_l[0] if per_group == 1 else jnp.concatenate(rows_l, 0)
                    term = product(first + i, rows_l)
                    total = term if total is None else total + term
                total = total * factor
                parts[g, t, turn] = total.astype(jnp.bfloat16)
                whole[g, t, turn] = total
                return carry

            lax.fori_loop(0, jnp.where(feeds, 2 * reps, reps), one_tile, 0)
            for j in range(1, orbs * reps):
                @pl.when(feeds)
                def _():
                    part_copy(g, 1, j).start()
            for j in range(1, orbs * reps):
                part_copy(g, 0, j).start()

    def summed(g, t):
        total = whole[g, t, r, pl.ds(o * rows_out, rows_out), :]
        for j in range(1, orbs * reps):
            part_copy(g, t, j).wait_recv()
            total = total + arrived[g, t, j - 1].astype(jnp.float32)
        return total

    def finish(g):
        @pl.when(inner)
        def _():
            @pl.when(feeds)
            def _():
                ends[g] = summed(g, 1)
                feed(g).start()

            pair_out[:, g * cols_group:(g + 1) * cols_group] = summed(g, 0)

    ahead = min(3, pieces)
    ready = 0
    closed = 0

    def one_occ(l, carry):
        occ[l] = jnp.dot(masked[l], occ_dens[...], preferred_element_type=jnp.float32).astype(jnp.bfloat16)
        return carry

    own(0)
    own(1)
    lax.fori_loop(0, batch, one_occ, 0)
    for c in range(min(ahead, pieces)):
        relay(c)
        end_occ(c)
    for c in range(pieces):
        if c + 2 < pieces:
            own(c + 2)
        if c + ahead < pieces:
            relay(c + ahead)
            end_occ(c + ahead)
        filled = c + ahead >= pieces - 1
        if filled and (ready + 1) * per_group <= c:
            group(ready)
            ready += 1
        complete(c)
        if c == 0:
            total = None
            for l in range(batch):
                term = product(l, masked[l, pl.ds(r * self_cols, self_cols), :])
                total = term if total is None else total + term
            self_tile[...] = total * factor
        if c == 1:
            for j in range(1, orbs):
                self_copy(j).start()
        if filled and c == pieces - 2 and closed + 1 < ready:
            finish(closed)
            closed += 1
        if filled and c < pieces - 1 and (ready + 1) * per_group <= c + 1:
            group(ready)
            ready += 1
    for g in range(ready, groups):
        group(g)
    total = self_tile[pl.ds(o * rows_out, rows_out), :]
    for j in range(1, orbs):
        self_copy(j).wait_recv()
        total = total + self_arrived[j - 1]
    self_out[...] = total
    for g in range(closed, groups):
        finish(g)

    @pl.when(at_end)
    def _():
        for g in range(groups):
            feed(g).wait_recv()
            pair_out[:, g * cols_group:(g + 1) * cols_group] = landed[g]

    for c in range(pieces):
        for d in range(chips):
            @pl.when(jnp.logical_and(up_ok, z - d >= 0))
            def _():
                up(c, jnp.maximum(z - d, 0), piece(c)).wait_send()

            @pl.when(jnp.logical_and(down_ok, z + d <= chips - 1))
            def _():
                down(c, jnp.minimum(z + d, chips - 1), piece(c)).wait_send()

        @pl.when(inner)
        def _():
            for zz in range(chips):
                cross(c, zz, piece(c)).wait_send()

    for j in range(1, orbs):
        self_copy(j).wait_send()
    for g in range(groups):
        @pl.when(inner)
        def _():
            for j in range(1, orbs * reps):
                part_copy(g, 0, j).wait_send()

        @pl.when(feeds)
        def _():
            for j in range(1, orbs * reps):
                part_copy(g, 1, j).wait_send()
            feed(g).wait_send()


def per_device(slab, occ_density, virt_density, block_mask, matching):
    owners = lax.axis_size("aux")
    orbs = lax.axis_size("orb")
    reps = lax.axis_size("rep")
    chips = owners // 2
    aux_rows, batch, orb_cols = slab.shape
    pieces = max(2, 32 // chips)
    rows_piece = aux_rows // pieces
    per_group = max(1, BLOCK // rows_piece)
    groups = pieces // per_group
    cols_group = per_group * rows_piece
    half = batch // reps
    rows_out = aux_rows // orbs
    self_cols = aux_rows // reps
    weights = block_mask.astype(jnp.bfloat16)
    spread = jnp.repeat(jnp.repeat(weights, BLOCK, axis=0), BLOCK, axis=1)
    masked = jnp.transpose(slab, (1, 0, 2)) * spread[None]
    factor = 1.0 / math.sqrt(batch * orb_cols * orbs)
    dma = pltpu.SemaphoreType.DMA
    vmem = pl.BlockSpec(memory_space=pltpu.VMEM)
    bf16, f32 = jnp.bfloat16, jnp.float32
    pair, own = pl.pallas_call(
        functools.partial(kernel, (chips, orbs, reps, pieces, groups, rows_piece, half), factor),
        out_shape=(
            jax.ShapeDtypeStruct((rows_out, aux_rows), f32),
            jax.ShapeDtypeStruct((rows_out, self_cols), f32),
        ),
        in_specs=[pl.BlockSpec(memory_space=pltpu.SMEM), vmem, vmem, vmem],
        out_specs=(vmem, vmem),
        scratch_shapes=[pltpu.VMEM((owners, half, rows_piece, orb_cols), bf16) for _ in range(pieces)] + [
            pltpu.VMEM((batch + half, aux_rows, orb_cols), bf16),
            pltpu.VMEM((groups, 2, reps, aux_rows, cols_group), bf16),
            pltpu.VMEM((groups, 2, reps, aux_rows, cols_group), f32),
            pltpu.VMEM((groups, 2, orbs * reps - 1, rows_out, cols_group), bf16),
            pltpu.VMEM((groups, rows_out, cols_group), f32),
            pltpu.VMEM((groups, rows_out, cols_group), f32),
            pltpu.VMEM((aux_rows, self_cols), f32),
            pltpu.VMEM((orbs - 1, rows_out, self_cols), f32),
            dma((pieces, chips)), dma((pieces, chips)), dma((pieces, chips)),
            dma((pieces, chips)), dma((pieces, chips)),
            dma((pieces,)), dma((groups,)), dma((groups,)),
            dma((groups, 2, orbs * reps - 1)), dma((groups, 2, orbs * reps - 1)),
            dma((orbs - 1,)), dma((orbs - 1,)),
        ],
        compiler_params=pltpu.CompilerParams(
            collective_id=0, has_side_effects=True, vmem_limit_bytes=56 * 2**20
        ),
    )(matching, masked, occ_density, virt_density)
    return (pair[None], own)


def solution(mesh):
    return jax.shard_map(
        per_device,
        mesh=mesh,
        in_specs=(P("aux", None, "orb"), P("orb", None), P("orb", None), P("aux", "orb"), P()),
        out_specs=(P("rep", ("aux", "orb"), None), P(("aux", "orb"), "rep")),
        check_vma=False,
    )
```
